128 devices in a mesh: row: 8 (over y, z_lo), col: 16 (over x, z_hi, core).
Axes of the slice: x: 4, y: 4, z: 4 (z_hi: 2, z_lo: 2; z = z_hi * 2 + z_lo), core: 2. Of those that a mesh axis runs over, the one named last changes fastest.
Arguments:
- returns: bfloat16 [32768, 256], P(('col', 'row')), may hold values from -6 to 6
- start_day: int32 [32768], P(('col', 'row')), may hold values from 0 to 127
- shrink_code: int32 [1], replicated, may hold values from 64 to 191
- weights: bfloat16 [32768, 512], P(('col', 'row')), may hold values from -1.5 to 1.5
Outputs:
- exposures: float32 [32768, 512], P(('col', 'row'))
The draws below stay inside these ranges and needn't reach their ends.
All inputs are finite; a program needn't handle non-finite values.
Results may differ from the reference program's by a relative error of at most 0.0041.
Values may be sent and summed in bfloat16 or wider, within the bound.
A program may use at most 128 MiB of HBM per device.

```python
import math
import jax
import jax.numpy as jnp
from jax import lax

TDAY = 256
PORT = 512
DENOM = 256
NASSET = 32768


def set_ends(entries, own_key, low, high):
    longest = entries.shape.index(max(entries.shape))
    spots = []
    for shift in (0, 1):
        where = [jax.random.randint(jax.random.fold_in(own_key, axis), (), 0, length) for axis, length in enumerate(entries.shape)]
        where[longest] = (where[longest] + shift) % entries.shape[longest]
        spots.append(tuple(where))
    return entries.at[spots[0]].set(low).at[spots[1]].set(high)


def shard_levels(key, shape, pieces, smallest, high):
    level = 1.0
    for position, shards_of in pieces:
        heights = jax.random.uniform(jax.random.fold_in(jax.random.fold_in(key, 6), position), (shards_of,), jnp.float32, smallest / len(pieces), high / len(pieces))
        level = level * jnp.repeat(jnp.exp(heights), shape[position] // shards_of).reshape((-1,) + (1,) * (len(shape) - 1 - position))
    return level


def scatter_about(stream_key, shape, scale, limit, cuts=(), kind=jnp.bfloat16):
    gain = shard_levels(stream_key, shape, cuts, -0.22, 0.18) if cuts else 1.0
    result = jax.random.normal(stream_key, shape, jnp.float32) * scale * gain
    return jnp.minimum(jnp.maximum(result, -limit), limit).astype(kind)


def setup_inputs(seed: int = 0) -> dict:
    key_list = jax.random.split(jax.random.key(seed), 5)
    return {
        "returns": scatter_about(key_list[0], (NASSET, TDAY), 1.0, 6.0, ((0, 128),)),
        "start_day": set_ends(jax.random.randint(key_list[1], (NASSET,), 0, TDAY // 2), jax.random.fold_in(key_list[1], 1), 0, (TDAY // 2) - 1).astype(jnp.int32),
        "shrink_code": jax.random.randint(key_list[2], (1,), 64, 192).astype(jnp.int32),
        "weights": scatter_about(key_list[3], (NASSET, PORT), 0.25, 1.5, ((0, 128),)),
    }


def reference(returns, start_day, shrink_code, weights):
    days = jnp.arange(TDAY, dtype=jnp.int32)
    listed = days[None, :] >= start_day[:, None]
    masked = jnp.where(listed, returns, jnp.zeros_like(returns)).astype(jnp.bfloat16)
    observed = (masked != 0).astype(jnp.bfloat16)
    squared = (masked.astype(jnp.float32) * masked.astype(jnp.float32)).astype(jnp.bfloat16)
    counts = lax.optimization_barrier(jnp.sum(observed.astype(jnp.float32), axis=1))
    sigma = jnp.sqrt(lax.optimization_barrier(jnp.sum(squared.astype(jnp.float32), axis=1)) / jnp.maximum(counts, 1.0) + 1e-06)
    scaled = (sigma[:, None] * weights.astype(jnp.float32)).astype(jnp.bfloat16)
    delta = shrink_code[0].astype(jnp.float32) / DENOM
    block_rows = math.gcd(NASSET, 512)
    col_ids = jnp.arange(NASSET, dtype=jnp.int32)

    def one_block(index):
        first = (index * block_rows).astype(jnp.int32)
        rows_y = lax.dynamic_slice_in_dim(masked, first, block_rows, 0)
        rows_o = lax.dynamic_slice_in_dim(observed, first, block_rows, 0)
        rows_s = lax.dynamic_slice_in_dim(squared, first, block_rows, 0)
        cross = jnp.dot(rows_y, masked.T, preferred_element_type=jnp.float32)
        left = jnp.dot(rows_s, observed.T, preferred_element_type=jnp.float32)
        right = jnp.dot(rows_o, squared.T, preferred_element_type=jnp.float32)
        corr = cross / jnp.sqrt(left * right + 1e-06)
        row_ids = first + jnp.arange(block_rows, dtype=jnp.int32)
        ident = (row_ids[:, None] == col_ids[None, :]).astype(jnp.float32)
        shrunk = ((1.0 - delta) * corr + delta * ident).astype(jnp.bfloat16)
        row_sigma = lax.dynamic_slice_in_dim(sigma, first, block_rows, 0)
        return row_sigma[:, None] * jnp.dot(shrunk, scaled, preferred_element_type=jnp.float32)
    blocks = lax.map(one_block, jnp.arange(NASSET // block_rows, dtype=jnp.int32))
    return blocks.reshape(NASSET, PORT)
```

```python
import functools

import jax
import jax.numpy as jnp
from jax import lax
from jax.experimental import pallas as pl
from jax.experimental.pallas import tpu as pltpu
from jax.sharding import PartitionSpec as P

DENOM = 256
MESH = pl.DeviceIdType.MESH
NT = (((1,), (1,)), ((), ()))
F32 = jnp.float32
BF16 = jnp.bfloat16


def flip1(v):
    return v + 1 - 2 * lax.rem(v, 2)


def flip3(v):
    return 3 - v


def peers():
    row = lax.axis_index("row")
    col = lax.axis_index("col")
    y, zl = lax.div(row, 2), lax.rem(row, 2)
    x, zh, core = lax.div(col, 4), lax.rem(lax.div(col, 2), 2), lax.rem(col, 2)
    z = zh * 2 + zl

    def device(x, y, z, core):
        return (y * 2 + lax.rem(z, 2), (x * 2 + lax.div(z, 2)) * 2 + core)

    def pick(first, second):
        return tuple(a * (1 - core) + b * core for a, b in zip(first, second))

    out = []
    for flip in (flip1, flip3):
        along_x = device(flip(x), y, z, core)
        along_y = device(x, flip(y), z, core)
        along_z = device(x, y, flip(z), core)
        out.append([pick(along_x, along_z), along_y, pick(along_z, along_x)])
    return out[0], out[1], device(x, y, z, 1 - core)


def kernel(
    ret_ref, start_ref, code_ref, w_ref, out_ref,
    yr, orow, srow, yc, oc, sc, v, s, diag, sig,
    sbuf, rbuf2, rbuf1, rbuf0,
    yc_send, yc_recv, yp_send, yp_recv, yr_send, yr_recv,
    v_send, v_recv, vp_send, vp_recv, o_send, o_recv,
):
    nb, days = ret_ref.shape
    half = w_ref.shape[1] // 2
    cbits, rbits, mate = peers()

    barrier = pltpu.get_barrier_semaphore()
    for peer in (*cbits, *rbits, mate):
        pl.semaphore_signal(barrier, inc=1, device_id=peer, device_id_type=MESH)

    starts = start_ref[...].reshape(1, nb).astype(F32)
    day = lax.broadcasted_iota(jnp.int32, (days, nb), 0).astype(F32)
    listed = jnp.where(day >= starts, 1.0, 0.0).astype(F32).T
    masked = jnp.where(listed > 0.5, ret_ref[...].astype(F32), 0.0)
    seen = jnp.where(masked != 0.0, 1.0, 0.0)
    squared = (masked * masked).astype(BF16).astype(F32)
    counts = jnp.sum(seen, axis=1, keepdims=True)
    sigma = jnp.sqrt(
        jnp.sum(squared, axis=1, keepdims=True) / jnp.maximum(counts, 1.0) + 1e-06
    )
    yr[0:nb, :] = masked.astype(BF16)
    yc[0:nb, :] = masked.astype(BF16)
    scaled = (sigma * w_ref[...].astype(F32)).astype(BF16)
    v[0, 0:nb, :] = scaled[:, :half]
    v[1, 0:nb, :] = scaled[:, half:]
    sig[...] = jnp.broadcast_to(sigma, sig.shape)
    delta = code_ref[0].astype(F32) / DENOM
    keep = 1.0 - delta

    pl.semaphore_wait(barrier, 7)

    def rows(pos, count=1):
        return pl.ds(pos * nb, count * nb)

    def yc_copy(m, bit):
        to = m + (1 << bit)
        return pltpu.make_async_remote_copy(
            src_ref=yc.at[rows(2 * m)], dst_ref=yc.at[rows(2 * to)],
            send_sem=yc_send.at[to], recv_sem=yc_recv.at[to],
            device_id=cbits[bit], device_id_type=MESH)

    def yp_copy(m):
        return pltpu.make_async_remote_copy(
            src_ref=yc.at[rows(2 * m)], dst_ref=yc.at[rows(2 * m + 1)],
            send_sem=yp_send.at[m], recv_sem=yp_recv.at[m],
            device_id=mate, device_id_type=MESH)

    def yr_copy(m, bit):
        to = m + (1 << bit)
        return pltpu.make_async_remote_copy(
            src_ref=yr.at[rows(m)], dst_ref=yr.at[rows(to)],
            send_sem=yr_send.at[to], recv_sem=yr_recv.at[to],
            device_id=rbits[bit], device_id_type=MESH)

    def v_copy(h, m, bit):
        to = m + (1 << bit)
        return pltpu.make_async_remote_copy(
            src_ref=v.at[h, rows(2 * m)], dst_ref=v.at[h, rows(2 * to)],
            send_sem=v_send.at[h, to], recv_sem=v_recv.at[h, to],
            device_id=cbits[bit], device_id_type=MESH)

    def vp_copy(h, m):
        return pltpu.make_async_remote_copy(
            src_ref=v.at[h, rows(2 * m)], dst_ref=v.at[h, rows(2 * m + 1)],
            send_sem=vp_send.at[h, m], recv_sem=vp_recv.at[h, m],
            device_id=mate, device_id_type=MESH)

    def bits_above(m):
        return [b for b in range(3) if (1 << b) > m]

    def last_bit(m):
        return m.bit_length() - 1

    def arrive(copy, m, forward):
        if m:
            b = last_bit(m)
            copy(m - (1 << b), b).wait_recv()
        for b in reversed(bits_above(m)):
            copy(m, b).start()
        if forward is not None:
            forward(m).start()

    def y_arrive(m):
        arrive(yc_copy, m, yp_copy)

    def r_arrive(m):
        arrive(yr_copy, m, None)

    def v_arrive(h, m):
        arrive(functools.partial(v_copy, h), m, functools.partial(vp_copy, h))

    def derive(y_ref, o_ref, s_ref, pos, count):
        def body(i, carry):
            r = pl.ds(pl.multiple_of((pos + i) * nb, nb), nb)
            y = y_ref[r, :]
            o_ref[r, :] = jnp.where(y != 0, 1.0, 0.0).astype(BF16)
            wide = y.astype(F32)
            s_ref[r, :] = (wide * wide).astype(BF16)
            return carry
        lax.fori_loop(0, count, body, 0)

    def corr_tile(r, c):
        cross = lax.dot_general(yr[r, :], yc[c, :], NT, preferred_element_type=F32)
        left = lax.dot_general(srow[r, :], oc[c, :], NT, preferred_element_type=F32)
        right = lax.dot_general(orow[r, :], sc[c, :], NT, preferred_element_type=F32)
        return cross * lax.rsqrt(left * right + 1e-06) * keep

    def corr_tiles(rpos, cchip, count):
        r = pl.ds(rpos * nb, 4 * nb)

        def body(i, carry):
            c = pl.ds(pl.multiple_of((cchip + i) * 2 * nb, 2 * nb), 2 * nb)
            s[r, c] = corr_tile(r, c).astype(BF16)
            return carry
        lax.fori_loop(0, count, body, 0)

    def apply_rows(h, pos):
        r = pl.ds(pl.multiple_of(pos * nb, nb), nb)
        return jnp.dot(s[r, :], v[h], preferred_element_type=F32)

    def o2_copy(h, i):
        return pltpu.make_async_remote_copy(
            src_ref=sbuf.at[h, 4 + i], dst_ref=rbuf2.at[h, i],
            send_sem=o_send.at[h, 4 + i], recv_sem=o_recv.at[h, 4 + i],
            device_id=rbits[2], device_id_type=MESH)

    def o1_copy(h, i):
        return pltpu.make_async_remote_copy(
            src_ref=sbuf.at[h, 2 + i], dst_ref=rbuf1.at[h, i],
            send_sem=o_send.at[h, 2 + i], recv_sem=o_recv.at[h, 2 + i],
            device_id=rbits[1], device_id_type=MESH)

    def o0_copy(h):
        return pltpu.make_async_remote_copy(
            src_ref=sbuf.at[h, 1], dst_ref=rbuf0.at[h],
            send_sem=o_send.at[h, 1], recv_sem=o_recv.at[h, 1],
            device_id=rbits[0], device_id_type=MESH)

    def group4(h):
        def body(i, carry):
            sbuf[h, 4 + i] = apply_rows(h, 4 + i).astype(BF16)
            o2_copy(h, i).start()
            return carry
        lax.fori_loop(0, 4, body, 0)

    def group2(h):
        def body(i, carry):
            part = apply_rows(h, 2 + i)
            o2_copy(h, 2 + i).wait_recv()
            sbuf[h, 2 + i] = (part + rbuf2[h, 2 + i].astype(F32)).astype(BF16)
            o1_copy(h, i).start()
            return carry
        lax.fori_loop(0, 2, body, 0)

    def group1(h):
        part = apply_rows(h, 1)
        o2_copy(h, 1).wait_recv()
        part = part + rbuf2[h, 1].astype(F32)
        o1_copy(h, 1).wait_recv()
        sbuf[h, 1] = (part + rbuf1[h, 1].astype(F32)).astype(BF16)
        o0_copy(h).start()

    def group0(h):
        part = apply_rows(h, 0)
        o2_copy(h, 0).wait_recv()
        part = part + rbuf2[h, 0].astype(F32)
        o1_copy(h, 0).wait_recv()
        out_ref[:, h * half:(h + 1) * half] = part + rbuf1[h, 0].astype(F32)

    def finish(h):
        o0_copy(h).wait_recv()
        cols = slice(h * half, (h + 1) * half)
        out_ref[:, cols] = (out_ref[:, cols] + rbuf0[h].astype(F32)) * sig[:, 0:1]

    y_arrive(0)
    r_arrive(0)
    derive(yr, orow, srow, 0, 1)
    derive(yc, oc, sc, 0, 1)
    own = rows(0)
    ident = (
        lax.broadcasted_iota(jnp.int32, (nb, nb), 0)
        == lax.broadcasted_iota(jnp.int32, (nb, nb), 1)
    ).astype(F32)
    diag[...] = (corr_tile(own, own) + delta * ident).astype(BF16)

    for m in (1, 2, 3):
        y_arrive(m)
        r_arrive(m)
    v_arrive(0, 0)
    derive(yr, orow, srow, 1, 3)
    for m in (0, 1, 2, 3):
        yp_copy(m).wait_recv()
    derive(yc, oc, sc, 1, 7)
    corr_tiles(0, 0, 4)
    s[0:nb, 0:nb] = diag[...]

    for m in (4, 5, 6, 7):
        y_arrive(m)
        r_arrive(m)
    for m in (1, 2, 3):
        v_arrive(0, m)
    v_arrive(1, 0)
    derive(yr, orow, srow, 4, 4)
    corr_tiles(4, 0, 4)
    for m in (4, 5, 6, 7):
        yp_copy(m).wait_recv()
    for m in (4, 5, 6, 7):
        v_arrive(0, m)
    for m in (1, 2, 3):
        v_arrive(1, m)
    derive(yc, oc, sc, 8, 8)
    corr_tiles(4, 4, 4)
    for m in range(8):
        vp_copy(0, m).wait_recv()
    group4(0)
    for m in (4, 5, 6, 7):
        v_arrive(1, m)
    corr_tiles(0, 4, 4)
    for m in range(8):
        vp_copy(1, m).wait_recv()
    group4(1)
    group2(0)
    group2(1)
    group1(0)
    group1(1)
    group0(0)
    group0(1)
    finish(0)
    finish(1)

    for to in range(1, 8):
        b = last_bit(to)
        m = to - (1 << b)
        yc_copy(m, b).wait_send()
        yr_copy(m, b).wait_send()
        for h in (0, 1):
            v_copy(h, m, b).wait_send()
    for m in range(8):
        yp_copy(m).wait_send()
        for h in (0, 1):
            vp_copy(h, m).wait_send()
    for h in (0, 1):
        for i in range(4):
            o2_copy(h, i).wait_send()
        for i in range(2):
            o1_copy(h, i).wait_send()
        o0_copy(h).wait_send()


def per_device(returns, start_day, shrink_code, weights):
    nb, days = returns.shape
    port = weights.shape[1]
    half = port // 2
    nr, nc = 8 * nb, 16 * nb
    vmem = pl.BlockSpec(memory_space=pltpu.VMEM)
    smem = pl.BlockSpec(memory_space=pltpu.SMEM)
    dma = pltpu.SemaphoreType.DMA
    return pl.pallas_call(
        kernel,
        out_shape=jax.ShapeDtypeStruct((nb, port), F32),
        in_specs=[vmem, vmem, smem, vmem],
        out_specs=vmem,
        scratch_shapes=[
            pltpu.VMEM((nr, days), BF16), pltpu.VMEM((nr, days), BF16), pltpu.VMEM((nr, days), BF16),
            pltpu.VMEM((nc, days), BF16), pltpu.VMEM((nc, days), BF16), pltpu.VMEM((nc, days), BF16),
            pltpu.VMEM((2, nc, half), BF16),
            pltpu.VMEM((nr, nc), BF16),
            pltpu.VMEM((nb, nb), BF16),
            pltpu.VMEM((nb, 128), F32),
            pltpu.VMEM((2, 8, nb, half), BF16),
            pltpu.VMEM((2, 4, nb, half), BF16),
            pltpu.VMEM((2, 2, nb, half), BF16),
            pltpu.VMEM((2, nb, half), BF16),
            dma((8,)), dma((8,)), dma((8,)), dma((8,)), dma((8,)), dma((8,)),
            dma((2, 8)), dma((2, 8)), dma((2, 8)), dma((2, 8)), dma((2, 8)), dma((2, 8)),
        ],
        compiler_params=pltpu.CompilerParams(
            collective_id=0, has_side_effects=True, vmem_limit_bytes=60 << 20
        ),
    )(returns, start_day.reshape(1, nb), shrink_code, weights)


def solution(mesh):
    in_specs = (P(("col", "row"), None), P(("col", "row")), P(), P(("col", "row"), None))
    out_specs = P(("col", "row"), None)
    return jax.shard_map(
        per_device, mesh=mesh, in_specs=in_specs, out_specs=out_specs, check_vma=False
    )
```

```python
import functools

import jax
import jax.numpy as jnp
from jax import lax
from jax.experimental import pallas as pl
from jax.experimental.pallas import tpu as pltpu
from jax.sharding import PartitionSpec as P

DENOM = 256
MESH = pl.DeviceIdType.MESH
NT = (((1,), (1,)), ((), ()))
F32 = jnp.float32
BF16 = jnp.bfloat16

MASKS = (0, 1, 2, 4, 3, 5, 6, 7)
PLACE = tuple(MASKS.index(m) for m in range(8))

ORDERS = ((0, 1, 2), (1, 2, 0), (2, 0, 1), (2, 1, 0))
PLAN = (
    "s01", "s11", "s12", "y1", "r1", "r2", "y4", "s02", "v01", "y2", "T00",
    "v11", "v12", "T01",
    "r3", "v05", "y3", "y5", "T02",
    "s04", "v02", "T12",
    "v03", "m1", "s14", "T11",
    "v15", "y7", "y6", "T10",
    "v04", "v13", "T13",
    "v16", "v06", "v07", "m0", "T03",
    "A05",
    "v17", "v14", "o05", "A07",
    "o17", "o07", "A03",
    "o13", "o03", "A17",
    "o37", "o27", "A06",
    "o16", "A15",
    "o25", "o35", "A16",
    "o36", "o06", "A13",
    "o15", "A02",
    "o33", "o26", "A04",
    "o23", "A01",
    "o12", "o14", "A11",
    "o02", "o01", "o21", "A14",
    "o11", "A00",
    "A12",
    "o32", "o24", "o04", "o22", "A10",
    "o34", "o31", "o00", "o10", "o20", "o30",
)


def flip1(v):
    return v + 1 - 2 * lax.rem(v, 2)


def flip3(v):
    return 3 - v


def peers():
    row = lax.axis_index("row")
    col = lax.axis_index("col")
    y, zl = lax.div(row, 2), lax.rem(row, 2)
    x, zh, core = lax.div(col, 4), lax.rem(lax.div(col, 2), 2), lax.rem(col, 2)
    z = zh * 2 + zl

    def device(x, y, z, core):
        return (y * 2 + lax.rem(z, 2), (x * 2 + lax.div(z, 2)) * 2 + core)

    def pick(first, second):
        return tuple(a * (1 - core) + b * core for a, b in zip(first, second))

    out = []
    for flip in (flip1, flip3):
        along_x = device(flip(x), y, z, core)
        along_y = device(x, flip(y), z, core)
        along_z = device(x, y, flip(z), core)
        out.append([pick(along_x, along_z), along_y, pick(along_z, along_x)])
    return out[0], out[1], device(x, y, z, 1 - core)


def last_bit(m):
    return m.bit_length() - 1


def stage_of(q, m):
    for k, b in enumerate(ORDERS[q]):
        if m >> b & 1:
            return k
    return 3


def kernel(
    ret_ref, start_ref, code_ref, w_ref, out_ref,
    yr, orow, srow, yc, oc, sc, v, s, diag, sig, part, sbuf, rbuf,
    yc_send, yc_recv, yp_send, yp_recv, yr_send, yr_recv,
    v_send, v_recv, vp_send, vp_recv, o_send, o_recv,
):
    nb, days = ret_ref.shape
    half = w_ref.shape[1] // 2
    quarter = half // 2
    cbits, rbits, mate = peers()

    barrier = pltpu.get_barrier_semaphore()
    for peer in (*cbits, *rbits, mate):
        pl.semaphore_signal(barrier, inc=1, device_id=peer, device_id_type=MESH)

    starts = start_ref[...].reshape(1, nb).astype(F32)
    day = lax.broadcasted_iota(jnp.int32, (days, nb), 0).astype(F32)
    listed = jnp.where(day >= starts, 1.0, 0.0).astype(F32).T
    masked = jnp.where(listed > 0.5, ret_ref[...].astype(F32), 0.0)
    yr[0:nb, :] = masked.astype(BF16)
    yc[0:nb, :] = masked.astype(BF16)
    delta = code_ref[0].astype(F32) / DENOM
    keep = 1.0 - delta

    pl.semaphore_wait(barrier, 7)

    def block(pos, count=1):
        return pl.ds(pos * nb, count * nb)

    def remote(src, dst, send, recv, peer):
        return pltpu.make_async_remote_copy(
            src_ref=src, dst_ref=dst, send_sem=send, recv_sem=recv,
            device_id=peer, device_id_type=MESH)

    def col(m, other=0):
        return block(2 * PLACE[m] + other)

    def yc_copy(to):
        b = last_bit(to)
        return remote(yc.at[col(to - (1 << b))], yc.at[col(to)],
                      yc_send.at[to], yc_recv.at[to], cbits[b])

    def yp_copy(m):
        return remote(yc.at[col(m)], yc.at[col(m, 1)], yp_send.at[m], yp_recv.at[m], mate)

    def yr_copy(to):
        b = last_bit(to)
        return remote(yr.at[block(PLACE[to - (1 << b)])], yr.at[block(PLACE[to])],
                      yr_send.at[to], yr_recv.at[to], rbits[b])

    def v_copy(h, to):
        b = last_bit(to)
        return remote(v.at[h, col(to - (1 << b))], v.at[h, col(to)],
                      v_send.at[h, to], v_recv.at[h, to], cbits[b])

    def vp_copy(h, m):
        return remote(v.at[h, col(m)], v.at[h, col(m, 1)], vp_send.at[h, m], vp_recv.at[h, m], mate)

    def o_copy(q, m):
        return remote(sbuf.at[q, m], rbuf.at[q, m], o_send.at[q, m], o_recv.at[q, m],
                      rbits[ORDERS[q][stage_of(q, m)]])

    def pass_on(copy, m):
        for b in (2, 1, 0):
            if (1 << b) > m:
                copy(m + (1 << b)).start()

    def derive(y_ref, o_ref, s_ref, pos):
        y = y_ref[block(pos), :]
        o_ref[block(pos), :] = jnp.where(y != 0, 1.0, 0.0).astype(BF16)
        s_ref[block(pos), :] = y * y

    have = {"rows": {0}, "cols": {0}, "waited": {0}, "weights": set()}

    def wait_row(m):
        if m not in have["waited"]:
            have["waited"].add(m)
            yr_copy(m).wait_recv()

    def need_tile(side, pair):
        for pos in range(4 * side, 4 * side + 4):
            if pos not in have["rows"]:
                have["rows"].add(pos)
                wait_row(MASKS[pos])
                derive(yr, orow, srow, pos)
        for pos in range(4 * pair, 4 * pair + 4):
            if pos not in have["cols"]:
                have["cols"].add(pos)
                if pos % 2:
                    yp_copy(MASKS[pos // 2]).wait_recv()
                derive(yc, oc, sc, pos)

    def corr_tile(side, pair):
        r = pl.ds(pl.multiple_of(side * 4 * nb, 4 * nb), 4 * nb)
        for k in range(4):
            c = pl.ds(pl.multiple_of(pair * 4 * nb + k * nb, nb), nb)
            cross = lax.dot_general(yr[r, :], yc[c, :], NT, preferred_element_type=F32)
            left = lax.dot_general(srow[r, :], oc[c, :], NT, preferred_element_type=F32)
            right = lax.dot_general(orow[r, :], sc[c, :], NT, preferred_element_type=F32)
            s[r, c] = (cross * lax.rsqrt(left * right + 1e-06) * keep).astype(BF16)

    def need_weights(h):
        if h not in have["weights"]:
            have["weights"].add(h)
            for other in range(8):
                vp_copy(h, other).wait_recv()

    def apply_rows(h, place):
        r = pl.ds(pl.multiple_of(place * nb, nb), nb)
        part[h, place] = jnp.dot(s[r, :], v[h], preferred_element_type=F32)

    def add_up(q, m):
        h, c = q // 2, pl.ds((q % 2) * quarter, quarter)
        k = stage_of(q, m)
        total = part[h, PLACE[m], :, c]
        for b in ORDERS[q][:k]:
            o_copy(q, m | (1 << b)).wait_recv()
            total = total + rbuf[q, m | (1 << b)].astype(F32)
        if k < 3:
            sbuf[q, m] = total.astype(BF16)
            o_copy(q, m).start()
        else:
            out_ref[:, q * quarter:(q + 1) * quarter] = total * sig[...]

    pass_on(yc_copy, 0)
    pass_on(yr_copy, 0)
    yp_copy(0).start()

    seen = jnp.where(masked != 0.0, 1.0, 0.0)
    squared = (masked * masked).astype(BF16)
    orow[0:nb, :] = seen.astype(BF16)
    oc[0:nb, :] = seen.astype(BF16)
    srow[0:nb, :] = squared
    sc[0:nb, :] = squared
    counts = jnp.sum(seen, axis=1, keepdims=True)
    sigma = jnp.sqrt(
        jnp.sum(squared.astype(F32), axis=1, keepdims=True) / jnp.maximum(counts, 1.0) + 1e-06
    )
    scaled = (sigma * w_ref[...].astype(F32)).astype(BF16)
    v[0, 0:nb, :] = scaled[:, :half]
    v[1, 0:nb, :] = scaled[:, half:]
    sig[...] = jnp.broadcast_to(sigma, sig.shape)

    own = block(0)
    cross = lax.dot_general(yr[own, :], yc[own, :], NT, preferred_element_type=F32)
    left = lax.dot_general(srow[own, :], oc[own, :], NT, preferred_element_type=F32)
    right = lax.dot_general(orow[own, :], sc[own, :], NT, preferred_element_type=F32)
    ident = (
        lax.broadcasted_iota(jnp.int32, (nb, nb), 0)
        == lax.broadcasted_iota(jnp.int32, (nb, nb), 1)
    ).astype(F32)
    diag[...] = (cross * lax.rsqrt(left * right + 1e-06) * keep + delta * ident).astype(BF16)

    def event(step):
        what, n = step[0], [int(d) for d in step[1:]]
        if what == "y":
            yc_copy(n[0]).wait_recv()
            pass_on(yc_copy, n[0])
            yp_copy(n[0]).start()
        elif what == "r":
            wait_row(n[0])
            pass_on(yr_copy, n[0])
        elif what == "v":
            h, m = n
            v_copy(h, m).wait_recv()
            pass_on(functools.partial(v_copy, h), m)
            vp_copy(h, m).start()
        elif what == "s":
            v_copy(*n).start()
        elif what == "m":
            vp_copy(n[0], 0).start()
        elif what == "o":
            add_up(*n)

    steps, before = {"T": [], "A": []}, []
    for step in PLAN:
        if step[0] in "TA":
            steps[step[0]].append((tuple(int(d) for d in step[1:]), before))
            before = []
        else:
            before.append(step)

    def entry(i, values):
        out = values[0]
        for k, value in enumerate(values[1:], 1):
            if value != values[k - 1]:
                out = jnp.where(i >= k, value, out)
        return out

    tiles = steps["T"]

    def tile_step(i, carry):
        for k, (where, events) in enumerate(tiles):
            @pl.when(i == k)
            def _(where=where, events=events, k=k):
                for step in events:
                    event(step)
                need_tile(*where)
                if k == 1:
                    s[0:nb, 0:nb] = diag[...]
        corr_tile(entry(i, [w[0] for w, _ in tiles]), entry(i, [w[1] for w, _ in tiles]))
        return carry

    lax.fori_loop(0, len(tiles), tile_step, 0)

    products = steps["A"]

    def product_step(i, carry):
        for k, ((h, m), events) in enumerate(products):
            def prepare(h=h, events=events):
                for step in events:
                    event(step)
                need_weights(h)
            if events or h not in have["weights"]:
                pl.when(i == k)(prepare)
        apply_rows(entry(i, [w[0] for w, _ in products]), entry(i, [PLACE[w[1]] for w, _ in products]))
        return carry

    lax.fori_loop(0, len(products), product_step, 0)
    for step in before:
        event(step)

    for to in range(1, 8):
        yc_copy(to).wait_send()
        yr_copy(to).wait_send()
        for h in (0, 1):
            v_copy(h, to).wait_send()
        for q in range(4):
            o_copy(q, to).wait_send()
    for m in range(8):
        yp_copy(m).wait_send()
        for h in (0, 1):
            vp_copy(h, m).wait_send()


def per_device(returns, start_day, shrink_code, weights):
    nb, days = returns.shape
    port = weights.shape[1]
    half, quarter = port // 2, port // 4
    nr, nc = 8 * nb, 16 * nb
    vmem = pl.BlockSpec(memory_space=pltpu.VMEM)
    smem = pl.BlockSpec(memory_space=pltpu.SMEM)
    dma = pltpu.SemaphoreType.DMA
    return pl.pallas_call(
        kernel,
        out_shape=jax.ShapeDtypeStruct((nb, port), F32),
        in_specs=[vmem, vmem, smem, vmem],
        out_specs=vmem,
        scratch_shapes=[
            pltpu.VMEM((nr, days), BF16), pltpu.VMEM((nr, days), BF16), pltpu.VMEM((nr, days), BF16),
            pltpu.VMEM((nc, days), BF16), pltpu.VMEM((nc, days), BF16), pltpu.VMEM((nc, days), BF16),
            pltpu.VMEM((2, nc, half), BF16),
            pltpu.VMEM((nr, nc), BF16),
            pltpu.VMEM((nb, nb), BF16),
            pltpu.VMEM((nb, quarter), F32),
            pltpu.VMEM((2, 8, nb, half), F32),
            pltpu.VMEM((4, 8, nb, quarter), BF16),
            pltpu.VMEM((4, 8, nb, quarter), BF16),
            dma((8,)), dma((8,)), dma((8,)), dma((8,)), dma((8,)), dma((8,)),
            dma((2, 8)), dma((2, 8)), dma((2, 8)), dma((2, 8)), dma((4, 8)), dma((4, 8)),
        ],
        compiler_params=pltpu.CompilerParams(
            collective_id=0, has_side_effects=True, vmem_limit_bytes=62 << 20
        ),
    )(returns, start_day.reshape(1, nb), shrink_code, weights)


def solution(mesh):
    in_specs = (P(("col", "row"), None), P(("col", "row")), P(), P(("col", "row"), None))
    out_specs = P(("col", "row"), None)
    return jax.shard_map(
        per_device, mesh=mesh, in_specs=in_specs, out_specs=out_specs, check_vma=False
    )
```

```python
import functools

import jax
import jax.numpy as jnp
from jax import lax
from jax.experimental import pallas as pl
from jax.experimental.pallas import tpu as pltpu
from jax.sharding import PartitionSpec as P

DENOM = 256
MESH = pl.DeviceIdType.MESH
NT = (((1,), (1,)), ((), ()))
F32 = jnp.float32
BF16 = jnp.bfloat16

MASKS = (0, 1, 2, 4, 3, 5, 6, 7)
PLACE = tuple(MASKS.index(m) for m in range(8))

ORDERS = ((1, 2, 0), (2, 0, 1), (2, 0, 1), (2, 1, 0))
PLAN = (
    "s02", "s01", "s11", "y01", "r01", "y14", "y02", "r11", "r02", "r12", "y11", "v01", "y04", "y12", "y03", "s14", "r03", "s12", "r13", "T00",
    "y13", "m1", "s04", "y15", "T01",
    "v03", "v11", "y06", "v02", "y16", "T11",
    "y07", "y05", "y17", "m0", "T10",
    "v12", "T13",
    "v05", "v13", "v04", "T12",
    "v15", "v06", "v07", "T03",
    "v16", "A03",
    "v14", "v17", "A07",
    "o17", "A06",
    "o16", "A05",
    "o15", "A16",
    "o26", "A17",
    "o37", "o27", "o07", "A13",
    "o36", "o06", "A15",
    "o13", "o03", "o35", "T02",
    "o25", "A02",
    "o02", "o23", "o05", "A04",
    "o14", "o33", "A14",
    "o24", "A12",
    "o12", "o04", "o34", "A11",
    "o21", "A10",
    "o32", "A01",
    "o01", "A00",
    "o22", "o11", "o31", "o00", "o10", "o20", "o30",
)


def flip1(v):
    return v + 1 - 2 * lax.rem(v, 2)


def flip3(v):
    return 3 - v


def peers():
    row = lax.axis_index("row")
    col = lax.axis_index("col")
    y, zl = lax.div(row, 2), lax.rem(row, 2)
    x, zh, core = lax.div(col, 4), lax.rem(lax.div(col, 2), 2), lax.rem(col, 2)
    z = zh * 2 + zl

    def device(x, y, z, core):
        return (y * 2 + lax.rem(z, 2), (x * 2 + lax.div(z, 2)) * 2 + core)

    def pick(first, second):
        return tuple(a * (1 - core) + b * core for a, b in zip(first, second))

    out = []
    for flip in (flip1, flip3):
        along_x = device(flip(x), y, z, core)
        along_y = device(x, flip(y), z, core)
        along_z = device(x, y, flip(z), core)
        out.append([pick(along_x, along_z), along_y, pick(along_z, along_x)])
    return out[0], out[1], device(x, y, z, 1 - core)


def last_bit(m):
    return m.bit_length() - 1


def stage_of(q, m):
    for k, b in enumerate(ORDERS[q]):
        if m >> b & 1:
            return k
    return 3


def kernel(
    ret_ref, start_ref, code_ref, w_ref, out_ref,
    yr, orow, srow, yc, oc, sc, v, s, diag, sig, part, sbuf, rbuf,
    yc_send, yc_recv, yp_send, yp_recv, yr_send, yr_recv,
    v_send, v_recv, vp_send, vp_recv, o_send, o_recv,
):
    nb, days = ret_ref.shape
    half = w_ref.shape[1] // 2
    quarter = half // 2
    cbits, rbits, mate = peers()

    barrier = pltpu.get_barrier_semaphore()
    for peer in (*cbits, *rbits, mate):
        pl.semaphore_signal(barrier, inc=1, device_id=peer, device_id_type=MESH)

    starts = start_ref[...].reshape(1, nb).astype(F32)
    day = lax.broadcasted_iota(jnp.int32, (days, nb), 0).astype(F32)
    listed = jnp.where(day >= starts, 1.0, 0.0).astype(F32).T
    masked = jnp.where(listed > 0.5, ret_ref[...].astype(F32), 0.0)
    yr[0:nb, :] = masked.astype(BF16)
    yc[0:nb, :] = masked.astype(BF16)
    delta = code_ref[0].astype(F32) / DENOM
    keep = 1.0 - delta

    pl.semaphore_wait(barrier, 7)

    def block(pos, count=1):
        return pl.ds(pos * nb, count * nb)

    def remote(src, dst, send, recv, peer):
        return pltpu.make_async_remote_copy(
            src_ref=src, dst_ref=dst, send_sem=send, recv_sem=recv,
            device_id=peer, device_id_type=MESH)

    def col_place(m, other=0):
        return 8 * (PLACE[m] // 4) + 4 * other + PLACE[m] % 4

    def col(m, other=0):
        return block(col_place(m, other))

    def piece(place, g):
        return pl.ds(place * nb + g * (nb // 2), nb // 2)

    def yc_copy(g, to):
        b = last_bit(to)
        return remote(yc.at[piece(col_place(to - (1 << b)), g)], yc.at[piece(col_place(to), g)],
                      yc_send.at[g, to], yc_recv.at[g, to], cbits[b])

    def yp_copy(g, m):
        return remote(yc.at[piece(col_place(m), g)], yc.at[piece(col_place(m, 1), g)],
                      yp_send.at[g, m], yp_recv.at[g, m], mate)

    def yr_copy(g, to):
        b = last_bit(to)
        return remote(yr.at[piece(PLACE[to - (1 << b)], g)], yr.at[piece(PLACE[to], g)],
                      yr_send.at[g, to], yr_recv.at[g, to], rbits[b])

    def v_copy(h, to):
        b = last_bit(to)
        return remote(v.at[h, col(to - (1 << b))], v.at[h, col(to)],
                      v_send.at[h, to], v_recv.at[h, to], cbits[b])

    def vp_copy(h, m):
        return remote(v.at[h, col(m)], v.at[h, col(m, 1)], vp_send.at[h, m], vp_recv.at[h, m], mate)

    def o_copy(q, m):
        return remote(sbuf.at[q, m], rbuf.at[q, m], o_send.at[q, m], o_recv.at[q, m],
                      rbits[ORDERS[q][stage_of(q, m)]])

    def pass_on(copy, m):
        for b in (2, 1, 0):
            if (1 << b) > m:
                copy(m + (1 << b)).start()

    def derive(y_ref, o_ref, s_ref, pos):
        y = y_ref[block(pos), :]
        o_ref[block(pos), :] = jnp.where(y != 0, 1.0, 0.0).astype(BF16)
        s_ref[block(pos), :] = y * y

    have = {"rows": {0}, "cols": {0}, "waited": {(0, 0), (1, 0)}, "weights": set()}

    def wait_row(g, m):
        if (g, m) not in have["waited"]:
            have["waited"].add((g, m))
            yr_copy(g, m).wait_recv()

    def need_tile(side, pair):
        for pos in range(4 * side, 4 * side + 4):
            if pos not in have["rows"]:
                have["rows"].add(pos)
                wait_row(0, MASKS[pos])
                wait_row(1, MASKS[pos])
                derive(yr, orow, srow, pos)
        for pos in range(4 * pair, 4 * pair + 4):
            if pos not in have["cols"]:
                have["cols"].add(pos)
                if pos // 4 % 2:
                    for g in (0, 1):
                        yp_copy(g, MASKS[4 * (pos // 8) + pos % 4]).wait_recv()
                derive(yc, oc, sc, pos)

    def corr_tile(side, pair):
        r = pl.ds(pl.multiple_of(side * 4 * nb, 4 * nb), 4 * nb)
        for k in range(4):
            c = pl.ds(pl.multiple_of(pair * 4 * nb + k * nb, nb), nb)
            cross = lax.dot_general(yr[r, :], yc[c, :], NT, preferred_element_type=F32)
            left = lax.dot_general(srow[r, :], oc[c, :], NT, preferred_element_type=F32)
            right = lax.dot_general(orow[r, :], sc[c, :], NT, preferred_element_type=F32)
            s[r, c] = (cross * lax.rsqrt(left * right + 1e-06) * keep).astype(BF16)

    def need_weights(h):
        if h not in have["weights"]:
            have["weights"].add(h)
            for other in range(8):
                vp_copy(h, other).wait_recv()

    def apply_rows(h, place):
        r = pl.ds(pl.multiple_of(place * nb, nb), nb)
        part[h, place] = jnp.dot(s[r, :], v[h], preferred_element_type=F32)

    def add_up(q, m):
        h, c = q // 2, pl.ds((q % 2) * quarter, quarter)
        k = stage_of(q, m)
        total = part[h, PLACE[m], :, c]
        for b in ORDERS[q][:k]:
            o_copy(q, m | (1 << b)).wait_recv()
            total = total + rbuf[q, m | (1 << b)].astype(F32)
        if k < 3:
            sbuf[q, m] = total.astype(BF16)
            o_copy(q, m).start()
        else:
            out_ref[:, q * quarter:(q + 1) * quarter] = total * sig[...]

    for g in (0, 1):
        pass_on(functools.partial(yc_copy, g), 0)
        yp_copy(g, 0).start()
        pass_on(functools.partial(yr_copy, g), 0)

    seen = jnp.where(masked != 0.0, 1.0, 0.0)
    squared = (masked * masked).astype(BF16)
    orow[0:nb, :] = seen.astype(BF16)
    oc[0:nb, :] = seen.astype(BF16)
    srow[0:nb, :] = squared
    sc[0:nb, :] = squared
    counts = jnp.sum(seen, axis=1, keepdims=True)
    sigma = jnp.sqrt(
        jnp.sum(squared.astype(F32), axis=1, keepdims=True) / jnp.maximum(counts, 1.0) + 1e-06
    )
    scaled = (sigma * w_ref[...].astype(F32)).astype(BF16)
    v[0, 0:nb, :] = scaled[:, :half]
    v[1, 0:nb, :] = scaled[:, half:]
    sig[...] = jnp.broadcast_to(sigma, sig.shape)

    own = block(0)
    cross = lax.dot_general(yr[own, :], yc[own, :], NT, preferred_element_type=F32)
    left = lax.dot_general(srow[own, :], oc[own, :], NT, preferred_element_type=F32)
    right = lax.dot_general(orow[own, :], sc[own, :], NT, preferred_element_type=F32)
    ident = (
        lax.broadcasted_iota(jnp.int32, (nb, nb), 0)
        == lax.broadcasted_iota(jnp.int32, (nb, nb), 1)
    ).astype(F32)
    diag[...] = (cross * lax.rsqrt(left * right + 1e-06) * keep + delta * ident).astype(BF16)

    def event(step):
        what, n = step[0], [int(d) for d in step[1:]]
        if what == "y":
            yc_copy(*n).wait_recv()
            pass_on(functools.partial(yc_copy, n[0]), n[1])
            yp_copy(*n).start()
        elif what == "r":
            wait_row(*n)
            pass_on(functools.partial(yr_copy, n[0]), n[1])
        elif what == "v":
            h, m = n
            v_copy(h, m).wait_recv()
            pass_on(functools.partial(v_copy, h), m)
            vp_copy(h, m).start()
        elif what == "s":
            v_copy(*n).start()
        elif what == "m":
            vp_copy(n[0], 0).start()
        elif what == "o":
            add_up(*n)

    runs, before = [], []
    for step in PLAN:
        if step[0] in "TA":
            if not runs or runs[-1][0] != step[0]:
                runs.append((step[0], []))
            runs[-1][1].append((tuple(int(d) for d in step[1:]), before))
            before = []
        else:
            before.append(step)

    def entry(i, values):
        out = values[0]
        for k, value in enumerate(values[1:], 1):
            if value != values[k - 1]:
                out = jnp.where(i >= k, value, out)
        return out

    def run_steps(kind, entries, first):
        firsts = [e[0] for e, _ in entries]
        seconds = [e[1] if kind == "T" else PLACE[e[1]] for e, _ in entries]

        def one(i, carry):
            for k, (where, events) in enumerate(entries):
                def prepare(where=where, events=events, k=k):
                    for step in events:
                        event(step)
                    if kind == "T":
                        need_tile(*where)
                    else:
                        need_weights(where[0])
                    if first and k == 1:
                        s[0:nb, 0:nb] = diag[...]
                pl.when(i == k)(prepare)
            if kind == "T":
                corr_tile(entry(i, firsts), entry(i, seconds))
            else:
                apply_rows(entry(i, firsts), entry(i, seconds))
            return carry

        lax.fori_loop(0, len(entries), one, 0)

    for n, (kind, entries) in enumerate(runs):
        run_steps(kind, entries, n == 0)
    for step in before:
        event(step)

    for to in range(1, 8):
        for h in (0, 1):
            yc_copy(h, to).wait_send()
            yr_copy(h, to).wait_send()
            v_copy(h, to).wait_send()
        for q in range(4):
            o_copy(q, to).wait_send()
    for m in range(8):
        for h in (0, 1):
            yp_copy(h, m).wait_send()
            vp_copy(h, m).wait_send()


def per_device(returns, start_day, shrink_code, weights):
    nb, days = returns.shape
    port = weights.shape[1]
    half, quarter = port // 2, port // 4
    nr, nc = 8 * nb, 16 * nb
    vmem = pl.BlockSpec(memory_space=pltpu.VMEM)
    smem = pl.BlockSpec(memory_space=pltpu.SMEM)
    dma = pltpu.SemaphoreType.DMA
    return pl.pallas_call(
        kernel,
        out_shape=jax.ShapeDtypeStruct((nb, port), F32),
        in_specs=[vmem, vmem, smem, vmem],
        out_specs=vmem,
        scratch_shapes=[
            pltpu.VMEM((nr, days), BF16), pltpu.VMEM((nr, days), BF16), pltpu.VMEM((nr, days), BF16),
            pltpu.VMEM((nc, days), BF16), pltpu.VMEM((nc, days), BF16), pltpu.VMEM((nc, days), BF16),
            pltpu.VMEM((2, nc, half), BF16),
            pltpu.VMEM((nr, nc), BF16),
            pltpu.VMEM((nb, nb), BF16),
            pltpu.VMEM((nb, quarter), F32),
            pltpu.VMEM((2, 8, nb, half), F32),
            pltpu.VMEM((4, 8, nb, quarter), BF16),
            pltpu.VMEM((4, 8, nb, quarter), BF16),
            dma((2, 8)), dma((2, 8)), dma((2, 8)), dma((2, 8)), dma((2, 8)), dma((2, 8)),
            dma((2, 8)), dma((2, 8)), dma((2, 8)), dma((2, 8)), dma((4, 8)), dma((4, 8)),
        ],
        compiler_params=pltpu.CompilerParams(
            collective_id=0, has_side_effects=True, vmem_limit_bytes=62 << 20
        ),
    )(returns, start_day.reshape(1, nb), shrink_code, weights)


def solution(mesh):
    in_specs = (P(("col", "row"), None), P(("col", "row")), P(), P(("col", "row"), None))
    out_specs = P(("col", "row"), None)
    return jax.shard_map(
        per_device, mesh=mesh, in_specs=in_specs, out_specs=out_specs, check_vma=False
    )
```

```python
import functools

import jax
import jax.numpy as jnp
from jax import lax
from jax.experimental import pallas as pl
from jax.experimental.pallas import tpu as pltpu
from jax.sharding import PartitionSpec as P

DENOM = 256
MESH = pl.DeviceIdType.MESH
NT = (((1,), (1,)), ((), ()))
F32 = jnp.float32
BF16 = jnp.bfloat16

MASKS = (0, 1, 2, 4, 3, 5, 6, 7)
PLACE = tuple(MASKS.index(m) for m in range(8))

ORDERS = ((0, 1, 2), (1, 2, 0), (2, 0, 1), (2, 1, 0))
PLAN = (
    "s01", "s11", "s12", "y1", "r1", "r2", "y4", "s02", "v01", "y2", "T00",
    "v11", "v12", "T01",
    "r3", "v05", "y3", "y5", "T02",
    "s04", "v02", "T12",
    "v03", "m1", "s14", "T11",
    "v15", "y7", "y6", "T10",
    "v04", "v13", "T13",
    "v16", "v06", "v07", "m0", "T03",
    "A05",
    "v17", "v14", "o05", "A07",
    "o17", "o07", "A03",
    "o13", "o03", "A17",
    "o37", "o27", "A06",
    "o16", "A15",
    "o25", "o35", "A16",
    "o36", "o06", "A13",
    "o15", "A02",
    "o33", "o26", "A04",
    "o23", "A01",
    "o12", "o14", "A11",
    "o02", "o01", "o21", "A14",
    "o11", "A00",
    "A12",
    "o32", "o24", "o04", "o22", "A10",
    "o34", "o31", "o00", "o10", "o20", "o30",
)


def flip1(v):
    return v + 1 - 2 * lax.rem(v, 2)


def flip3(v):
    return 3 - v


def peers():
    row = lax.axis_index("row")
    col = lax.axis_index("col")
    y, zl = lax.div(row, 2), lax.rem(row, 2)
    x, zh, core = lax.div(col, 4), lax.rem(lax.div(col, 2), 2), lax.rem(col, 2)
    z = zh * 2 + zl

    def device(x, y, z, core):
        return (y * 2 + lax.rem(z, 2), (x * 2 + lax.div(z, 2)) * 2 + core)

    def pick(first, second):
        return tuple(a * (1 - core) + b * core for a, b in zip(first, second))

    out = []
    for flip in (flip3, flip1):
        along_x = device(flip(x), y, z, core)
        along_y = device(x, flip(y), z, core)
        along_z = device(x, y, flip(z), core)
        out.append([pick(along_x, along_z), along_y, pick(along_z, along_x)])
    return out[0], out[1], device(x, y, z, 1 - core)


def last_bit(m):
    return m.bit_length() - 1


def stage_of(q, m):
    for k, b in enumerate(ORDERS[q]):
        if m >> b & 1:
            return k
    return 3


def kernel(
    ret_ref, start_ref, code_ref, w_ref, out_ref,
    yr, orow, srow, yc, oc, sc, v, s, diag, sig, part, sbuf, rbuf,
    yc_send, yc_recv, yp_send, yp_recv, yr_send, yr_recv,
    v_send, v_recv, vp_send, vp_recv, o_send, o_recv,
):
    nb, days = ret_ref.shape
    half = w_ref.shape[1] // 2
    quarter = half // 2
    cbits, rbits, mate = peers()

    barrier = pltpu.get_barrier_semaphore()
    for peer in (*cbits, *rbits, mate):
        pl.semaphore_signal(barrier, inc=1, device_id=peer, device_id_type=MESH)

    starts = start_ref[...].reshape(1, nb).astype(F32)
    day = lax.broadcasted_iota(jnp.int32, (days, nb), 0).astype(F32)
    listed = jnp.where(day >= starts, 1.0, 0.0).astype(F32).T
    masked = jnp.where(listed > 0.5, ret_ref[...].astype(F32), 0.0)
    yr[0:nb, :] = masked.astype(BF16)
    yc[0:nb, :] = masked.astype(BF16)
    delta = code_ref[0].astype(F32) / DENOM
    keep = 1.0 - delta

    pl.semaphore_wait(barrier, 7)

    def block(pos, count=1):
        return pl.ds(pos * nb, count * nb)

    def remote(src, dst, send, recv, peer):
        return pltpu.make_async_remote_copy(
            src_ref=src, dst_ref=dst, send_sem=send, recv_sem=recv,
            device_id=peer, device_id_type=MESH)

    def col(m, other=0):
        return block(2 * PLACE[m] + other)

    def yc_copy(to):
        b = last_bit(to)
        return remote(yc.at[col(to - (1 << b))], yc.at[col(to)],
                      yc_send.at[to], yc_recv.at[to], cbits[b])

    def yp_copy(m):
        return remote(yc.at[col(m)], yc.at[col(m, 1)], yp_send.at[m], yp_recv.at[m], mate)

    def yr_copy(to):
        b = last_bit(to)
        return remote(yr.at[block(PLACE[to - (1 << b)])], yr.at[block(PLACE[to])],
                      yr_send.at[to], yr_recv.at[to], rbits[b])

    def v_copy(h, to):
        b = last_bit(to)
        return remote(v.at[h, col(to - (1 << b))], v.at[h, col(to)],
                      v_send.at[h, to], v_recv.at[h, to], cbits[b])

    def vp_copy(h, m):
        return remote(v.at[h, col(m)], v.at[h, col(m, 1)], vp_send.at[h, m], vp_recv.at[h, m], mate)

    def o_copy(q, m):
        return remote(sbuf.at[q, m], rbuf.at[q, m], o_send.at[q, m], o_recv.at[q, m],
                      rbits[ORDERS[q][stage_of(q, m)]])

    def pass_on(copy, m):
        for b in (2, 1, 0):
            if (1 << b) > m:
                copy(m + (1 << b)).start()

    def derive(y_ref, o_ref, s_ref, pos):
        y = y_ref[block(pos), :]
        o_ref[block(pos), :] = jnp.where(y != 0, 1.0, 0.0).astype(BF16)
        s_ref[block(pos), :] = y * y

    have = {"rows": {0}, "cols": {0}, "waited": {0}, "weights": set()}

    def wait_row(m):
        if m not in have["waited"]:
            have["waited"].add(m)
            yr_copy(m).wait_recv()

    def need_tile(side, pair):
        for pos in range(4 * side, 4 * side + 4):
            if pos not in have["rows"]:
                have["rows"].add(pos)
                wait_row(MASKS[pos])
                derive(yr, orow, srow, pos)
        for pos in range(4 * pair, 4 * pair + 4):
            if pos not in have["cols"]:
                have["cols"].add(pos)
                if pos % 2:
                    yp_copy(MASKS[pos // 2]).wait_recv()
                derive(yc, oc, sc, pos)

    def corr_tile(side, pair):
        r = pl.ds(pl.multiple_of(side * 4 * nb, 4 * nb), 4 * nb)
        for k in range(4):
            c = pl.ds(pl.multiple_of(pair * 4 * nb + k * nb, nb), nb)
            cross = lax.dot_general(yr[r, :], yc[c, :], NT, preferred_element_type=F32)
            left = lax.dot_general(srow[r, :], oc[c, :], NT, preferred_element_type=F32)
            right = lax.dot_general(orow[r, :], sc[c, :], NT, preferred_element_type=F32)
            s[r, c] = (cross * lax.rsqrt(left * right + 1e-06) * keep).astype(BF16)

    def need_weights(h):
        if h not in have["weights"]:
            have["weights"].add(h)
            for other in range(8):
                vp_copy(h, other).wait_recv()

    def apply_rows(h, place):
        r = pl.ds(pl.multiple_of(place * nb, nb), nb)
        part[h, place] = jnp.dot(s[r, :], v[h], preferred_element_type=F32)

    def add_up(q, m):
        h, c = q // 2, pl.ds((q % 2) * quarter, quarter)
        k = stage_of(q, m)
        total = part[h, PLACE[m], :, c]
        for b in ORDERS[q][:k]:
            o_copy(q, m | (1 << b)).wait_recv()
            total = total + rbuf[q, m | (1 << b)].astype(F32)
        if k < 3:
            sbuf[q, m] = total.astype(BF16)
            o_copy(q, m).start()
        else:
            out_ref[:, q * quarter:(q + 1) * quarter] = total * sig[...]

    pass_on(yc_copy, 0)
    pass_on(yr_copy, 0)
    yp_copy(0).start()

    seen = jnp.where(masked != 0.0, 1.0, 0.0)
    squared = (masked * masked).astype(BF16)
    orow[0:nb, :] = seen.astype(BF16)
    oc[0:nb, :] = seen.astype(BF16)
    srow[0:nb, :] = squared
    sc[0:nb, :] = squared
    counts = jnp.sum(seen, axis=1, keepdims=True)
    sigma = jnp.sqrt(
        jnp.sum(squared.astype(F32), axis=1, keepdims=True) / jnp.maximum(counts, 1.0) + 1e-06
    )
    scaled = (sigma * w_ref[...].astype(F32)).astype(BF16)
    v[0, 0:nb, :] = scaled[:, :half]
    v[1, 0:nb, :] = scaled[:, half:]
    sig[...] = jnp.broadcast_to(sigma, sig.shape)

    own = block(0)
    cross = lax.dot_general(yr[own, :], yc[own, :], NT, preferred_element_type=F32)
    left = lax.dot_general(srow[own, :], oc[own, :], NT, preferred_element_type=F32)
    right = lax.dot_general(orow[own, :], sc[own, :], NT, preferred_element_type=F32)
    ident = (
        lax.broadcasted_iota(jnp.int32, (nb, nb), 0)
        == lax.broadcasted_iota(jnp.int32, (nb, nb), 1)
    ).astype(F32)
    diag[...] = (cross * lax.rsqrt(left * right + 1e-06) * keep + delta * ident).astype(BF16)

    def event(step):
        what, n = step[0], [int(d) for d in step[1:]]
        if what == "y":
            yc_copy(n[0]).wait_recv()
            pass_on(yc_copy, n[0])
            yp_copy(n[0]).start()
        elif what == "r":
            wait_row(n[0])
            pass_on(yr_copy, n[0])
        elif what == "v":
            h, m = n
            v_copy(h, m).wait_recv()
            pass_on(functools.partial(v_copy, h), m)
            vp_copy(h, m).start()
        elif what == "s":
            v_copy(*n).start()
        elif what == "m":
            vp_copy(n[0], 0).start()
        elif what == "o":
            add_up(*n)

    steps, before = {"T": [], "A": []}, []
    for step in PLAN:
        if step[0] in "TA":
            steps[step[0]].append((tuple(int(d) for d in step[1:]), before))
            before = []
        else:
            before.append(step)

    def entry(i, values):
        out = values[0]
        for k, value in enumerate(values[1:], 1):
            if value != values[k - 1]:
                out = jnp.where(i >= k, value, out)
        return out

    tiles = steps["T"]

    def tile_step(i, carry):
        for k, (where, events) in enumerate(tiles):
            @pl.when(i == k)
            def _(where=where, events=events, k=k):
                for step in events:
                    event(step)
                need_tile(*where)
                if k == 1:
                    s[0:nb, 0:nb] = diag[...]
        corr_tile(entry(i, [w[0] for w, _ in tiles]), entry(i, [w[1] for w, _ in tiles]))
        return carry

    lax.fori_loop(0, len(tiles), tile_step, 0)

    products = steps["A"]

    def product_step(i, carry):
        for k, ((h, m), events) in enumerate(products):
            def prepare(h=h, events=events):
                for step in events:
                    event(step)
                need_weights(h)
            if events or h not in have["weights"]:
                pl.when(i == k)(prepare)
        apply_rows(entry(i, [w[0] for w, _ in products]), entry(i, [PLACE[w[1]] for w, _ in products]))
        return carry

    lax.fori_loop(0, len(products), product_step, 0)
    for step in before:
        event(step)

    for to in range(1, 8):
        yc_copy(to).wait_send()
        yr_copy(to).wait_send()
        for h in (0, 1):
            v_copy(h, to).wait_send()
        for q in range(4):
            o_copy(q, to).wait_send()
    for m in range(8):
        yp_copy(m).wait_send()
        for h in (0, 1):
            vp_copy(h, m).wait_send()


def per_device(returns, start_day, shrink_code, weights):
    nb, days = returns.shape
    port = weights.shape[1]
    half, quarter = port // 2, port // 4
    nr, nc = 8 * nb, 16 * nb
    vmem = pl.BlockSpec(memory_space=pltpu.VMEM)
    smem = pl.BlockSpec(memory_space=pltpu.SMEM)
    dma = pltpu.SemaphoreType.DMA
    return pl.pallas_call(
        kernel,
        out_shape=jax.ShapeDtypeStruct((nb, port), F32),
        in_specs=[vmem, vmem, smem, vmem],
        out_specs=vmem,
        scratch_shapes=[
            pltpu.VMEM((nr, days), BF16), pltpu.VMEM((nr, days), BF16), pltpu.VMEM((nr, days), BF16),
            pltpu.VMEM((nc, days), BF16), pltpu.VMEM((nc, days), BF16), pltpu.VMEM((nc, days), BF16),
            pltpu.VMEM((2, nc, half), BF16),
            pltpu.VMEM((nr, nc), BF16),
            pltpu.VMEM((nb, nb), BF16),
            pltpu.VMEM((nb, quarter), F32),
            pltpu.VMEM((2, 8, nb, half), F32),
            pltpu.VMEM((4, 8, nb, quarter), BF16),
            pltpu.VMEM((4, 8, nb, quarter), BF16),
            dma((8,)), dma((8,)), dma((8,)), dma((8,)), dma((8,)), dma((8,)),
            dma((2, 8)), dma((2, 8)), dma((2, 8)), dma((2, 8)), dma((4, 8)), dma((4, 8)),
        ],
        compiler_params=pltpu.CompilerParams(
            collective_id=0, has_side_effects=True, vmem_limit_bytes=62 << 20
        ),
    )(returns, start_day.reshape(1, nb), shrink_code, weights)


def solution(mesh):
    in_specs = (P(("col", "row"), None), P(("col", "row")), P(), P(("col", "row"), None))
    out_specs = P(("col", "row"), None)
    return jax.shard_map(
        per_device, mesh=mesh, in_specs=in_specs, out_specs=out_specs, check_vma=False
    )
```

```python
import functools

import jax
import jax.numpy as jnp
from jax import lax
from jax.experimental import pallas as pl
from jax.experimental.pallas import tpu as pltpu
from jax.sharding import PartitionSpec as P

DENOM = 256
MESH = pl.DeviceIdType.MESH
NT = (((1,), (1,)), ((), ()))
F32 = jnp.float32
BF16 = jnp.bfloat16

MASKS = (0, 1, 2, 4, 3, 5, 6, 7)
PLACE = tuple(MASKS.index(m) for m in range(8))

ORDERS = ((0, 1, 2), (1, 2, 0), (2, 0, 1), (2, 1, 0))
PLAN = (
    "s01", "s11", "s12", "y1", "r1", "r2", "y4", "s02", "v01", "y2", "T00",
    "v11", "v12", "T01",
    "r3", "v05", "y3", "y5", "T02",
    "s04", "v02", "T12",
    "v03", "m1", "s14", "T11",
    "v15", "y7", "y6", "T10",
    "v04", "v13", "T13",
    "v16", "v06", "v07", "m0", "T03",
    "A05",
    "v17", "v14", "o05", "A07",
    "o17", "o07", "A03",
    "o13", "o03", "A17",
    "o37", "o27", "A06",
    "o16", "A15",
    "o25", "o35", "A16",
    "o36", "o06", "A13",
    "o15", "A02",
    "o33", "o26", "A04",
    "o23", "A01",
    "o12", "o14", "A11",
    "o02", "o01", "o21", "A14",
    "o11", "A00",
    "A12",
    "o32", "o24", "o04", "o22", "A10",
    "o34", "o31", "o00", "o10", "o20", "o30",
)


def flip1(v):
    return v + 1 - 2 * lax.rem(v, 2)


def flip3(v):
    return 3 - v


def peers():
    row = lax.axis_index("row")
    col = lax.axis_index("col")
    y, zl = lax.div(row, 2), lax.rem(row, 2)
    x, zh, core = lax.div(col, 4), lax.rem(lax.div(col, 2), 2), lax.rem(col, 2)
    z = zh * 2 + zl

    def device(x, y, z, core):
        return (y * 2 + lax.rem(z, 2), (x * 2 + lax.div(z, 2)) * 2 + core)

    def pick(first, second):
        return tuple(a * (1 - core) + b * core for a, b in zip(first, second))

    out = []
    for flip in (flip3, flip1):
        along_x = device(flip(x), y, z, core)
        along_y = device(x, flip(y), z, core)
        along_z = device(x, y, flip(z), core)
        out.append([pick(along_x, along_z), along_y, pick(along_z, along_x)])
    return out[0], out[1], device(x, y, z, 1 - core)


def last_bit(m):
    return m.bit_length() - 1


def stage_of(q, m):
    for k, b in enumerate(ORDERS[q]):
        if m >> b & 1:
            return k
    return 3


def kernel(
    ret_ref, start_ref, code_ref, w_hbm, out_ref,
    yr, orow, srow, yc, oc, sc, v, s, diag, sig, part, sbuf, rbuf,
    yc_send, yc_recv, yp_send, yp_recv, yr_send, yr_recv,
    v_send, v_recv, vp_send, vp_recv, o_send, o_recv, w_ref, w_sem,
):
    nb, days = ret_ref.shape
    half = w_ref.shape[1] // 2
    quarter = half // 2
    cbits, rbits, mate = peers()
    w_copy = pltpu.make_async_copy(w_hbm, w_ref, w_sem)
    w_copy.start()

    barrier = pltpu.get_barrier_semaphore()
    for peer in (*cbits, *rbits, mate):
        pl.semaphore_signal(barrier, inc=1, device_id=peer, device_id_type=MESH)

    starts = start_ref[...].reshape(1, nb).astype(F32)
    day = lax.broadcasted_iota(jnp.int32, (days, nb), 0).astype(F32)
    listed = jnp.where(day >= starts, 1.0, 0.0).astype(F32).T
    masked = jnp.where(listed > 0.5, ret_ref[...].astype(F32), 0.0)
    yr[0:nb, :] = masked.astype(BF16)
    yc[0:nb, :] = masked.astype(BF16)
    delta = code_ref[0].astype(F32) / DENOM
    keep = 1.0 - delta

    pl.semaphore_wait(barrier, 7)

    def block(pos, count=1):
        return pl.ds(pos * nb, count * nb)

    def remote(src, dst, send, recv, peer):
        return pltpu.make_async_remote_copy(
            src_ref=src, dst_ref=dst, send_sem=send, recv_sem=recv,
            device_id=peer, device_id_type=MESH)

    def col(m, other=0):
        return block(2 * PLACE[m] + other)

    def yc_copy(to):
        b = last_bit(to)
        return remote(yc.at[col(to - (1 << b))], yc.at[col(to)],
                      yc_send.at[to], yc_recv.at[to], cbits[b])

    def yp_copy(m):
        return remote(yc.at[col(m)], yc.at[col(m, 1)], yp_send.at[m], yp_recv.at[m], mate)

    def yr_copy(to):
        b = last_bit(to)
        return remote(yr.at[block(PLACE[to - (1 << b)])], yr.at[block(PLACE[to])],
                      yr_send.at[to], yr_recv.at[to], rbits[b])

    def v_copy(h, to):
        b = last_bit(to)
        return remote(v.at[h, col(to - (1 << b))], v.at[h, col(to)],
                      v_send.at[h, to], v_recv.at[h, to], cbits[b])

    def vp_copy(h, m):
        return remote(v.at[h, col(m)], v.at[h, col(m, 1)], vp_send.at[h, m], vp_recv.at[h, m], mate)

    def o_copy(q, m):
        return remote(sbuf.at[q, m], rbuf.at[q, m], o_send.at[q, m], o_recv.at[q, m],
                      rbits[ORDERS[q][stage_of(q, m)]])

    def pass_on(copy, m):
        for b in (2, 1, 0):
            if (1 << b) > m:
                copy(m + (1 << b)).start()

    def derive(y_ref, o_ref, s_ref, pos):
        y = y_ref[block(pos), :]
        o_ref[block(pos), :] = jnp.where(y != 0, 1.0, 0.0).astype(BF16)
        s_ref[block(pos), :] = y * y

    have = {"rows": {0}, "cols": {0}, "waited": {0}, "weights": set()}

    def wait_row(m):
        if m not in have["waited"]:
            have["waited"].add(m)
            yr_copy(m).wait_recv()

    def need_tile(side, pair):
        for pos in range(4 * side, 4 * side + 4):
            if pos not in have["rows"]:
                have["rows"].add(pos)
                wait_row(MASKS[pos])
                derive(yr, orow, srow, pos)
        for pos in range(4 * pair, 4 * pair + 4):
            if pos not in have["cols"]:
                have["cols"].add(pos)
                if pos % 2:
                    yp_copy(MASKS[pos // 2]).wait_recv()
                derive(yc, oc, sc, pos)

    def corr_tile(side, pair):
        r = pl.ds(pl.multiple_of(side * 4 * nb, 4 * nb), 4 * nb)
        for k in range(4):
            c = pl.ds(pl.multiple_of(pair * 4 * nb + k * nb, nb), nb)
            cross = lax.dot_general(yr[r, :], yc[c, :], NT, preferred_element_type=F32)
            left = lax.dot_general(srow[r, :], oc[c, :], NT, preferred_element_type=F32)
            right = lax.dot_general(orow[r, :], sc[c, :], NT, preferred_element_type=F32)
            s[r, c] = (cross * lax.rsqrt(left * right + 1e-06) * keep).astype(BF16)

    def need_weights(h):
        if h not in have["weights"]:
            have["weights"].add(h)
            for other in range(8):
                vp_copy(h, other).wait_recv()

    def apply_rows(h, place):
        r = pl.ds(pl.multiple_of(place * nb, nb), nb)
        part[h, place] = jnp.dot(s[r, :], v[h], preferred_element_type=F32)

    def add_up(q, m):
        h, c = q // 2, pl.ds((q % 2) * quarter, quarter)
        k = stage_of(q, m)
        total = part[h, PLACE[m], :, c]
        for b in ORDERS[q][:k]:
            o_copy(q, m | (1 << b)).wait_recv()
            total = total + rbuf[q, m | (1 << b)].astype(F32)
        if k < 3:
            sbuf[q, m] = total.astype(BF16)
            o_copy(q, m).start()
        else:
            out_ref[:, q * quarter:(q + 1) * quarter] = total * sig[...]

    pass_on(yc_copy, 0)
    pass_on(yr_copy, 0)
    yp_copy(0).start()

    seen = jnp.where(masked != 0.0, 1.0, 0.0)
    squared = (masked * masked).astype(BF16)
    orow[0:nb, :] = seen.astype(BF16)
    oc[0:nb, :] = seen.astype(BF16)
    srow[0:nb, :] = squared
    sc[0:nb, :] = squared
    counts = jnp.sum(seen, axis=1, keepdims=True)
    sigma = jnp.sqrt(
        jnp.sum(squared.astype(F32), axis=1, keepdims=True) / jnp.maximum(counts, 1.0) + 1e-06
    )
    w_copy.wait()
    scaled = (sigma * w_ref[...].astype(F32)).astype(BF16)
    v[0, 0:nb, :] = scaled[:, :half]
    v[1, 0:nb, :] = scaled[:, half:]
    sig[...] = jnp.broadcast_to(sigma, sig.shape)

    own = block(0)
    cross = lax.dot_general(yr[own, :], yc[own, :], NT, preferred_element_type=F32)
    left = lax.dot_general(srow[own, :], oc[own, :], NT, preferred_element_type=F32)
    right = lax.dot_general(orow[own, :], sc[own, :], NT, preferred_element_type=F32)
    ident = (
        lax.broadcasted_iota(jnp.int32, (nb, nb), 0)
        == lax.broadcasted_iota(jnp.int32, (nb, nb), 1)
    ).astype(F32)
    diag[...] = (cross * lax.rsqrt(left * right + 1e-06) * keep + delta * ident).astype(BF16)

    def event(step):
        what, n = step[0], [int(d) for d in step[1:]]
        if what == "y":
            yc_copy(n[0]).wait_recv()
            pass_on(yc_copy, n[0])
            yp_copy(n[0]).start()
        elif what == "r":
            wait_row(n[0])
            pass_on(yr_copy, n[0])
        elif what == "v":
            h, m = n
            v_copy(h, m).wait_recv()
            pass_on(functools.partial(v_copy, h), m)
            vp_copy(h, m).start()
        elif what == "s":
            v_copy(*n).start()
        elif what == "m":
            vp_copy(n[0], 0).start()
        elif what == "o":
            add_up(*n)

    steps, before = {"T": [], "A": []}, []
    for step in PLAN:
        if step[0] in "TA":
            steps[step[0]].append((tuple(int(d) for d in step[1:]), before))
            before = []
        else:
            before.append(step)

    def entry(i, values):
        out = values[0]
        for k, value in enumerate(values[1:], 1):
            if value != values[k - 1]:
                out = jnp.where(i >= k, value, out)
        return out

    tiles = steps["T"]

    def tile_step(i, carry):
        for k, (where, events) in enumerate(tiles):
            @pl.when(i == k)
            def _(where=where, events=events, k=k):
                for step in events:
                    event(step)
                need_tile(*where)
                if k == 1:
                    s[0:nb, 0:nb] = diag[...]
        corr_tile(entry(i, [w[0] for w, _ in tiles]), entry(i, [w[1] for w, _ in tiles]))
        return carry

    lax.fori_loop(0, len(tiles), tile_step, 0)

    products = steps["A"]

    def product_step(i, carry):
        for k, ((h, m), events) in enumerate(products):
            def prepare(h=h, events=events):
                for step in events:
                    event(step)
                need_weights(h)
            if events or h not in have["weights"]:
                pl.when(i == k)(prepare)
        apply_rows(entry(i, [w[0] for w, _ in products]), entry(i, [PLACE[w[1]] for w, _ in products]))
        return carry

    lax.fori_loop(0, len(products), product_step, 0)
    for step in before:
        event(step)

    for to in range(1, 8):
        yc_copy(to).wait_send()
        yr_copy(to).wait_send()
        for h in (0, 1):
            v_copy(h, to).wait_send()
        for q in range(4):
            o_copy(q, to).wait_send()
    for m in range(8):
        yp_copy(m).wait_send()
        for h in (0, 1):
            vp_copy(h, m).wait_send()


def per_device(returns, start_day, shrink_code, weights):
    nb, days = returns.shape
    port = weights.shape[1]
    half, quarter = port // 2, port // 4
    nr, nc = 8 * nb, 16 * nb
    vmem = pl.BlockSpec(memory_space=pltpu.VMEM)
    smem = pl.BlockSpec(memory_space=pltpu.SMEM)
    dma = pltpu.SemaphoreType.DMA
    return pl.pallas_call(
        kernel,
        out_shape=jax.ShapeDtypeStruct((nb, port), F32),
        in_specs=[vmem, vmem, smem, pl.BlockSpec(memory_space=pl.ANY)],
        out_specs=vmem,
        scratch_shapes=[
            pltpu.VMEM((nr, days), BF16), pltpu.VMEM((nr, days), BF16), pltpu.VMEM((nr, days), BF16),
            pltpu.VMEM((nc, days), BF16), pltpu.VMEM((nc, days), BF16), pltpu.VMEM((nc, days), BF16),
            pltpu.VMEM((2, nc, half), BF16),
            pltpu.VMEM((nr, nc), BF16),
            pltpu.VMEM((nb, nb), BF16),
            pltpu.VMEM((nb, quarter), F32),
            pltpu.VMEM((2, 8, nb, half), F32),
            pltpu.VMEM((4, 8, nb, quarter), BF16),
            pltpu.VMEM((4, 8, nb, quarter), BF16),
            dma((8,)), dma((8,)), dma((8,)), dma((8,)), dma((8,)), dma((8,)),
            dma((2, 8)), dma((2, 8)), dma((2, 8)), dma((2, 8)), dma((4, 8)), dma((4, 8)),
            pltpu.VMEM((nb, port), BF16), dma,
        ],
        compiler_params=pltpu.CompilerParams(
            collective_id=0, has_side_effects=True, vmem_limit_bytes=62 << 20
        ),
    )(returns, start_day.reshape(1, nb), shrink_code, weights)


def solution(mesh):
    in_specs = (P(("col", "row"), None), P(("col", "row")), P(), P(("col", "row"), None))
    out_specs = P(("col", "row"), None)
    return jax.shard_map(
        per_device, mesh=mesh, in_specs=in_specs, out_specs=out_specs, check_vma=False
    )
```
